128 devices in a mesh: gx: 8 (over y, core), gy: 16 (over z, x).
Axes of the slice: x: 4, y: 4, z: 4, core: 2. Of those that a mesh axis runs over, the one named last changes fastest.
Arguments:
- face_block: float32 [8, 16, 4, 512, 512], P('gx', 'gy'), may hold values from -40 to 40, as said below
- coupling: float32 [8, 16, 4, 512, 1024], P('gx', 'gy'), may hold values from -1.1 to 1.1
- interior_inverse: float32 [8, 16, 1024, 1024], P('gx', 'gy'), may hold values from -5 to 5, as said below
- face_values: float32 [8, 16, 4, 512, 128], P('gx', 'gy'), may hold values from -6 to 6
- adjacency: int32 [8, 16, 4], P('gx', 'gy'), may hold values from 0 to 1, as said below
- primal_basis: float32 [8, 16, 2048, 384], P('gx', 'gy'), may hold values from -0.125 to 0.125
- primal_matrix: float32 [8, 16, 384, 384], P('gx', 'gy'), may hold values from -0.15625 to 0.15625
- primal_map: int32 [8, 16, 384], P('gx', 'gy'), may hold values from 0 to 16383, as said below
- primal_count: int32 [8, 16], P('gx', 'gy'), may hold values from 128 to 384, as said below
Outputs:
- averaged: float32 [8, 16, 4, 512, 128], P('gx', 'gy')
- coarse_product: float32 [16384, 128], P(('gx', 'gy'))
The draws below stay inside these ranges and needn't reach their ends.
Inputs may be any that keep to these rules, and one draw needn't show every extreme that they name: `adjacency`: equal on both sides of every face and 0 on the faces at the grid's outer boundary. `primal_map`: coarse rows (a 16 + b) * 128 to (a 16 + b + 1) * 128 - 1 form the block of the subdomain at grid position (a, b). Every row of the subdomain at (i, j) lies in the block of the subdomain at (i, j), (i - 1, j), (i, j - 1) or (i - 1, j - 1); its rows below primal_count are distinct. `primal_count`: at most 128 times the number of the blocks named for primal_map that lie inside the grid; some subdomain has exactly 384 live primal unknowns. interior_inverse is symmetric positive definite. face_block is symmetric, and face_block minus the condensed interior term is positive definite.
All inputs are finite; a program needn't handle non-finite values.
Results may differ from the reference program's by a relative error of at most 0.000062.
Values sent between devices are 32-bit elements; how exact they have to be, the bound alone decides.
A program may use at most 128 MiB of HBM per device.

```python
import math
import jax
import jax.numpy as jnp
from jax import lax

F = 512
NI = 1024
FACES = 4
RHS = 128
PRIMAL = 384
CB = 128
NX = 8
NY = 16
NC = 16384


def interior_draw(key):
    key_one, key_two = jax.random.split(jax.random.fold_in(key, 11))
    factor_draw = jnp.clip(jax.random.normal(key_one, (NX * NY, NI, NI), jnp.float32), -3.0, 3.0)
    diag_part = jnp.exp(jax.random.uniform(key_two, (NX * NY, NI), jnp.float32, math.log(0.05), math.log(0.5)))

    def one_gram(factor_mat):
        gram = jnp.dot(factor_mat, factor_mat.T, precision=lax.Precision.HIGHEST, preferred_element_type=jnp.float32)
        return 0.25 * (gram + gram.T) / NI
    gram_all = lax.map(one_gram, factor_draw)
    eye_mat = jnp.eye(NI, dtype=jnp.float32)
    return (gram_all + diag_part[:, :, None] * eye_mat).reshape(NX, NY, NI, NI)


def coupling_draw(key):
    key_one = jax.random.fold_in(jax.random.fold_in(key, 37), 0)
    noise_draw = jnp.clip(jax.random.normal(key_one, (NX, NY, FACES, F, NI), jnp.float32), -3.0, 3.0) / math.sqrt(NI)
    return noise_draw


def draw_interior_inverse(key, part):
    return interior_draw(key)


def draw_coupling(key, part):
    return coupling_draw(key)


def draw_face_block(key, part):
    sub_count = NX * NY
    inverse_all = interior_draw(key).reshape(sub_count, NI, NI)
    couple_all = coupling_draw(key).reshape(sub_count, FACES, F, NI)
    key_one, key_two = jax.random.split(jax.random.fold_in(key, 23), 2)
    factor_draw = jnp.clip(jax.random.normal(key_one, (sub_count, FACES, F, F), jnp.float32), -3.0, 3.0)
    scale_draw = jnp.ones((sub_count, FACES, F), jnp.float32)
    diag_part = jnp.exp(jax.random.uniform(key_two, (sub_count, FACES, F), jnp.float32, math.log(0.1), math.log(1.0)))
    eye_mat = jnp.eye(F, dtype=jnp.float32)

    def one_subdomain(entry_set):
        factor_mat, diag_vals, scale_vals, couple_mat, inverse_mat = entry_set
        gram = jnp.einsum('fab,fcb->fac', factor_mat, factor_mat, precision=lax.Precision.HIGHEST) * (0.5 / F)
        base_part = gram + diag_vals[:, :, None] * eye_mat
        base_part = base_part * scale_vals[:, :, None] * scale_vals[:, None, :]
        left_part = jnp.einsum('fan,nm->fam', couple_mat, inverse_mat, precision=lax.Precision.HIGHEST)
        condensed = jnp.einsum('fam,fbm->fab', left_part, couple_mat, precision=lax.Precision.HIGHEST)
        summed = base_part + condensed
        return 0.5 * (summed + jnp.swapaxes(summed, -1, -2))
    blocks_all = lax.map(one_subdomain, (factor_draw, diag_part, scale_draw, couple_all, inverse_all))
    return blocks_all.reshape(NX, NY, FACES, F, F)


def draw_adjacency(key, part):
    key_one, key_two = jax.random.split(jax.random.fold_in(key, 41))
    glue_x = (jax.random.randint(key_one, (NX, NY), 0, 5) > 0).astype(jnp.int32)
    glue_y = (jax.random.randint(key_two, (NX, NY), 0, 5) > 0).astype(jnp.int32)
    zero_x = jnp.zeros((1, NY), jnp.int32)
    zero_y = jnp.zeros((NX, 1), jnp.int32)
    lower_x = jnp.concatenate([zero_x, glue_x[:-1]], axis=0)
    upper_x = jnp.concatenate([glue_x[:-1], zero_x], axis=0)
    lower_y = jnp.concatenate([zero_y, glue_y[:, :-1]], axis=1)
    upper_y = jnp.concatenate([glue_y[:, :-1], zero_y], axis=1)
    return jnp.stack([lower_x, upper_x, lower_y, upper_y], axis=-1)


def primal_layout(key):
    base_key = jax.random.fold_in(key, 61)
    perm_key, count_key, pick_key = jax.random.split(base_key, 3)
    sub_count = NX * NY
    sub_ids = jnp.arange(sub_count, dtype=jnp.int32)
    grid_row = sub_ids // NY
    grid_col = sub_ids % NY
    slot_ids = jnp.arange(4 * CB, dtype=jnp.int32)
    step_x = slot_ids // (2 * CB)
    step_y = slot_ids // CB % 2
    offset = slot_ids % CB
    inside = (grid_row[:, None] - step_x[None, :] >= 0) & (grid_col[:, None] - step_y[None, :] >= 0)
    shuffled = jax.vmap(lambda one_key: jax.random.permutation(one_key, 4 * CB))(jax.random.split(perm_key, sub_count)).astype(jnp.int32)
    scores = (1 - inside.astype(jnp.int32)) * (4 * CB) + shuffled
    chosen = jnp.argsort(scores, axis=1, stable=True)[:, :PRIMAL].astype(jnp.int32)
    chosen_inside = jnp.take_along_axis(inside, chosen, axis=1)
    block_row = jnp.where(chosen_inside, grid_row[:, None] - step_x[chosen], grid_row[:, None])
    block_col = jnp.where(chosen_inside, grid_col[:, None] - step_y[chosen], grid_col[:, None])
    rows_map = (block_row * NY + block_col) * CB + offset[chosen]
    capacity = CB * (1 + (grid_row > 0).astype(jnp.int32)) * (1 + (grid_col > 0).astype(jnp.int32))
    drawn_count = jax.random.randint(count_key, (sub_count,), PRIMAL // 2, PRIMAL + 1)
    counts_all = jnp.minimum(drawn_count, capacity)
    pick_index = jax.random.randint(pick_key, (), 0, (NX - 1) * (NY - 1))
    forced = (1 + pick_index // (NY - 1)) * NY + 1 + pick_index % (NY - 1)
    counts_all = jnp.where(sub_ids == forced, PRIMAL, counts_all)
    return (rows_map.reshape(NX, NY, PRIMAL).astype(jnp.int32), counts_all.reshape(NX, NY).astype(jnp.int32))


def draw_primal_map(key, part):
    return primal_layout(key)[0]


def draw_primal_count(key, part):
    return primal_layout(key)[1]


def steps_of(rng, shape, shards, least, largest):
    def one(dim, shards_of):
        draws = jax.random.uniform(jax.random.fold_in(jax.random.fold_in(rng, 6), dim), (shards_of,), jnp.float32, least / len(shards), largest / len(shards))
        return jnp.repeat(jnp.exp(draws), shape[dim] // shards_of).reshape((-1,) + (1,) * (len(shape) - dim - 1))

    factor_of = one(*shards[0])
    for cut in shards[1:]:
        factor_of = factor_of * one(*cut)
    return factor_of


def scatter_about(rng, shape, deviation, bound, shards=(), kind=jnp.bfloat16):
    level = steps_of(rng, shape, shards, -0.22, 0.18) if shards else 1.0
    drawn = jax.random.normal(rng, shape, jnp.float32) * deviation * level
    return jnp.minimum(jnp.maximum(drawn, -bound), bound).astype(kind)


def setup_inputs(seed: int = 0) -> dict:
    key_of = jax.random.split(jax.random.key(seed), 10)
    return {
        "face_block": draw_face_block(jax.random.fold_in(key_of[9], 71), 0),
        "coupling": draw_coupling(jax.random.fold_in(key_of[9], 71), 0),
        "interior_inverse": draw_interior_inverse(jax.random.fold_in(key_of[9], 71), 0),
        "face_values": scatter_about(key_of[3], (NX, NY, FACES, F, RHS), 1.0, 6.0, ((0, 8), (1, 16)), jnp.float32),
        "adjacency": draw_adjacency(jax.random.fold_in(key_of[9], 71), 0),
        "primal_basis": scatter_about(key_of[5], (NX, NY, FACES * F, PRIMAL), (FACES * F) ** -0.5, 0.125, ((0, 8), (1, 16)), jnp.float32),
        "primal_matrix": scatter_about(key_of[6], (NX, NY, PRIMAL, PRIMAL), (4 * PRIMAL) ** -0.5, 0.15625, ((0, 8), (1, 16)), jnp.float32),
        "primal_map": draw_primal_map(jax.random.fold_in(key_of[9], 71), 0),
        "primal_count": draw_primal_count(jax.random.fold_in(key_of[9], 71), 0),
    }


def condense(blocks, couple, inverse, values):
    face_count, face_size, inner_size = couple.shape
    left_part = jnp.dot(couple.reshape(face_count * face_size, inner_size).astype(jnp.float32), inverse.astype(jnp.float32), precision=lax.Precision.HIGHEST, preferred_element_type=jnp.float32)
    left_part = left_part.reshape(face_count, face_size, inner_size)
    schur_block = blocks - jnp.einsum('fan,fbn->fab', left_part, couple, precision=lax.Precision.HIGHEST)
    weighted = jnp.einsum('fab,fbr->far', schur_block, values, precision=lax.Precision.HIGHEST)
    return (schur_block, weighted)

def deluxe_solve(summed_matrix, rhs_side):
    factor = jnp.linalg.cholesky(summed_matrix)
    inner_part = lax.linalg.triangular_solve(factor, rhs_side, left_side=True, lower=True)
    return lax.linalg.triangular_solve(factor, inner_part, left_side=True, lower=True, transpose_a=True)

def reference(face_block, coupling, interior_inverse, face_values, adjacency, primal_basis, primal_matrix, primal_map, primal_count):
    sub_count = NX * NY
    schur_block, weighted = lax.map(lambda entry_set: condense(*entry_set), (face_block.reshape(sub_count, FACES, F, F), coupling.reshape(sub_count, FACES, F, NI), interior_inverse.reshape(sub_count, NI, NI), face_values.reshape(sub_count, FACES, F, RHS)))
    schur_block = schur_block.reshape(NX, NY, FACES, F, F)
    weighted = weighted.reshape(NX, NY, FACES, F, RHS)
    packed = jnp.concatenate([schur_block, weighted], axis=-1)
    pack_width = F + RHS
    zero_x = jnp.zeros((1, NY, F, pack_width), jnp.float32)
    zero_y = jnp.zeros((NX, 1, F, pack_width), jnp.float32)
    lower_x = jnp.concatenate([zero_x, packed[:-1, :, 1]], axis=0)
    upper_x = jnp.concatenate([packed[1:, :, 0], zero_x], axis=0)
    lower_y = jnp.concatenate([zero_y, packed[:, :-1, 3]], axis=1)
    upper_y = jnp.concatenate([packed[:, 1:, 2], zero_y], axis=1)
    across = jnp.stack([lower_x, upper_x, lower_y, upper_y], axis=2)
    across = across * adjacency.astype(jnp.float32)[..., None, None]
    summed_matrix = schur_block + across[..., :F]
    rhs_side = weighted + across[..., F:]
    averaged = lax.map(lambda entry_set: deluxe_solve(*entry_set), (summed_matrix.reshape(sub_count, FACES, F, F), rhs_side.reshape(sub_count, FACES, F, RHS)))
    averaged = averaged.reshape(NX, NY, FACES, F, RHS)
    live_mask = (jnp.arange(PRIMAL, dtype=jnp.int32)[None, :] < primal_count.reshape(sub_count, 1)).astype(jnp.float32)[..., None]
    primal = jnp.einsum('dkp,dkr->dpr', primal_basis.reshape(sub_count, FACES * F, PRIMAL), averaged.reshape(sub_count, FACES * F, RHS), precision=lax.Precision.HIGHEST) * live_mask
    row_index = primal_map.reshape(sub_count * PRIMAL).astype(jnp.int32)
    coarse_residual = jnp.zeros((NC, RHS), jnp.float32).at[row_index].add(primal.reshape(sub_count * PRIMAL, RHS))
    picked = coarse_residual[row_index].reshape(sub_count, PRIMAL, RHS) * live_mask
    local_terms = jnp.einsum('dpq,dqr->dpr', primal_matrix.reshape(sub_count, PRIMAL, PRIMAL), picked, precision=lax.Precision.HIGHEST) * live_mask
    coarse_product = jnp.zeros((NC, RHS), jnp.float32).at[row_index].add(local_terms.reshape(sub_count * PRIMAL, RHS))
    return (averaged, coarse_product)
```

```python
import functools

import jax
import jax.numpy as jnp
from jax import lax
from jax.experimental import pallas as pl
from jax.experimental.pallas import tpu as pltpu
from jax.sharding import PartitionSpec as P

CB = 128
TILE = 256
NB = 128
F32 = jnp.float32
BF16 = jnp.bfloat16
NN = (((1,), (0,)), ((), ()))
NT = (((1,), (1,)), ((), ()))
TN = (((0,), (0,)), ((), ()))


def halves(x):
    hi = x.astype(BF16)
    lo = (x - hi.astype(F32)).astype(BF16)
    return hi, lo


def mul(a, b, dims):
    return lax.dot_general(a, b, dims, preferred_element_type=F32)


def dot3(a, b, dims=NN):
    ah, al = a if isinstance(a, tuple) else halves(a)
    bh, bl = b if isinstance(b, tuple) else halves(b)
    return mul(ah, bh, dims) + (mul(ah, bl, dims) + mul(al, bh, dims))


def schur_of(a, c_hi, c_lo, t_hi, t_lo, size, width, acc):
    for j in range(width // TILE):
        cols = slice(j * TILE, (j + 1) * TILE)
        rest = slice(j * TILE, width)
        w = dot3((c_hi[:, rest], c_lo[:, rest]), (t_hi[rest, cols], t_lo[rest, cols]))
        part = dot3(w, (c_hi[:, cols], c_lo[:, cols]), NT)
        if j == 0:
            acc[...] = part
        else:
            acc[...] += part
    x = acc[...]
    return a - (x + x.T)


def split_inverse(k_ref, t_hi, t_lo):
    n = k_ref.shape[-1]
    for i in range(n // TILE):
        for j in range(i + 1):
            rows, cols = slice(i * TILE, (i + 1) * TILE), slice(j * TILE, (j + 1) * TILE)
            t = k_ref[rows, cols]
            if i == j:
                t = 0.5 * t
            t_hi[rows, cols], t_lo[rows, cols] = halves(t)


def schur_kernel(with_rhs, faces_ref, c_ref, k_ref, a_ref, *rest):
    if with_rhs:
        v_ref, nb_ref, s_ref, rhs_ref, t_hi, t_lo, c_hi, c_lo, acc = rest
    else:
        s_ref, t_hi, t_lo, c_hi, c_lo, acc = rest

    @pl.when(pl.program_id(0) == 0)
    def _():
        split_inverse(k_ref, t_hi, t_lo)

    c_hi[...], c_lo[...] = halves(c_ref[0])
    size, width = c_ref.shape[1:]
    s = schur_of(a_ref[0], c_hi, c_lo, t_hi, t_lo, size, width, acc)
    s_ref[0] = s
    if with_rhs:
        rhs_ref[0] = dot3(s, v_ref[0] - nb_ref[0])


def schur_call(faces, couple, inverse, blocks, values=None, nb_values=None):
    _, size, width = couple.shape
    with_rhs = values is not None
    pick = lambda g, f: (f[g], 0, 0)
    in_specs = [
        pl.BlockSpec((1, size, width), pick),
        pl.BlockSpec((width, width), lambda g, f: (0, 0), pipeline_mode=pl.Buffered(1)),
        pl.BlockSpec((1, size, size), pick),
    ]
    out_shape = [jax.ShapeDtypeStruct((2, size, size), F32)]
    out_specs = [pl.BlockSpec((1, size, size), lambda g, f: (g, 0, 0))]
    operands = [faces, couple, inverse, blocks]
    if with_rhs:
        rhs_count = values.shape[-1]
        in_specs += [
            pl.BlockSpec((1, size, rhs_count), pick),
            pl.BlockSpec((1, size, rhs_count), lambda g, f: (g, 0, 0)),
        ]
        out_shape.append(jax.ShapeDtypeStruct((2, size, rhs_count), F32))
        out_specs.append(pl.BlockSpec((1, size, rhs_count), lambda g, f: (g, 0, 0)))
        operands += [values, nb_values]
    flops = 2 * (2 * size * width * width * 3 + 2 * size * size * width * 3)
    return pl.pallas_call(
        functools.partial(schur_kernel, with_rhs),
        grid_spec=pltpu.PrefetchScalarGridSpec(
            num_scalar_prefetch=1,
            grid=(2,),
            in_specs=in_specs,
            out_specs=out_specs,
            scratch_shapes=[
                pltpu.VMEM((width, width), BF16),
                pltpu.VMEM((width, width), BF16),
                pltpu.VMEM((size, width), BF16),
                pltpu.VMEM((size, width), BF16),
                pltpu.VMEM((size, size), F32),
            ],
        ),
        out_shape=out_shape,
        name="schur_keep" if with_rhs else "schur_send",
        cost_estimate=pl.CostEstimate(
            flops=flops, bytes_accessed=4 * width * width + 2 * 4 * size * (width + 2 * size), transcendentals=0
        ),
    )(*operands)


def lane(x, k, shape):
    return jnp.broadcast_to(x[:, k : k + 1], shape)


def sub(x, k, shape):
    return jnp.broadcast_to(x[k : k + 1, :], shape)


def invert_blocks(blocks):
    n = blocks[0].shape[0]
    tile = (8, n)
    rows = lax.broadcasted_iota(jnp.int32, tile, 0)
    cols = lax.broadcasted_iota(jnp.int32, tile, 1)
    mats = [[b[8 * q : 8 * q + 8, :] for q in range(n // 8)] for b in blocks]
    for p in range(n // 8):
        lanes = (cols >= 8 * p) & (cols < 8 * p + 8)
        unit = jnp.where(cols - 8 * p == rows, 1.0, 0.0).astype(F32)
        for mat in mats:
            tile_p = mat[p]
            c = [lane(tile_p, 8 * p + j, tile) for j in range(8)]
            u = jnp.where(lanes, unit, tile_p)
            for j in range(8):
                r = 1.0 / sub(c[j], j, tile)
                f = jnp.where(rows == j, 1.0 - r, c[j] * r)
                u = u - f * sub(u, j, tile)
                for m in range(j + 1, 8):
                    c[m] = c[m] - f * sub(c[m], j, tile)
            u_rows = [sub(u, j, tile) for j in range(8)]
            for q in range(n // 8):
                if q == p:
                    continue
                t = mat[q]
                acc = jnp.where(lanes, 0.0, t)
                for j in range(8):
                    acc = acc - lane(t, 8 * p + j, tile) * u_rows[j]
                mat[q] = acc
            mat[p] = u
    return [jnp.concatenate(m, axis=0) for m in mats]


def solve_kernel(adj_ref, s_ref, t_ref, rhs_ref, v_ref, nb_ref, x_ref, m_ref, b_ref):
    size = s_ref.shape[1]
    count = size // NB
    m_ref[...] = s_ref[...] + t_ref[...]
    b_ref[...] = rhs_ref[...]
    for k in range(count):
        rk = slice(k * NB, (k + 1) * NB)
        inv = invert_blocks([m_ref[f, rk, rk] for f in range(2)])
        for f in range(2):
            d = halves(inv[f])
            vb = halves(dot3(d, b_ref[f, rk, :]))
            if k < count - 1:
                vm = halves(dot3(d, m_ref[f, rk, (k + 1) * NB :]))
                m_ref[f, rk, (k + 1) * NB :] = vm[0].astype(F32) + vm[1].astype(F32)
            for i in range(count):
                ri = slice(i * NB, (i + 1) * NB)
                if i == k:
                    continue
                left = halves(m_ref[f, ri, rk])
                b_ref[f, ri, :] -= dot3(left, vb)
                if k < count - 1:
                    m_ref[f, ri, (k + 1) * NB :] -= dot3(left, vm)
            b_ref[f, rk, :] = vb[0].astype(F32) + vb[1].astype(F32)
    for f in range(2):
        x_ref[f] = jnp.where(adj_ref[f] > 0, nb_ref[f] + b_ref[f], v_ref[f])


def solve_call(adj, s, t, rhs, v, nb):
    _, size, width = rhs.shape
    full = pl.BlockSpec(memory_space=pltpu.VMEM)
    return pl.pallas_call(
        solve_kernel,
        in_specs=[pl.BlockSpec(memory_space=pltpu.SMEM)] + [full] * 5,
        out_specs=full,
        out_shape=jax.ShapeDtypeStruct((2, size, width), F32),
        scratch_shapes=[pltpu.VMEM((2, size, size), F32), pltpu.VMEM((2, size, width), F32)],
        name="solve",
        cost_estimate=pl.CostEstimate(flops=10**10, bytes_accessed=6 << 20, transcendentals=0),
    )(adj, s, t, rhs, v, nb)


def hi3(a, b, dims=NN):
    return lax.dot_general(
        a, b, dims, precision=lax.Precision.HIGH, preferred_element_type=F32
    )


def shards(
    face_block,
    coupling,
    interior_inverse,
    face_values,
    adjacency,
    primal_basis,
    primal_matrix,
    primal_map,
    primal_count,
):
    nx, ny = lax.axis_size("gx"), lax.axis_size("gy")
    ix, iy = lax.axis_index("gx"), lax.axis_index("gy")
    odd = ix % 2
    axes = ("gx", "gy")

    def shift(x, move):
        pairs = []
        for i in range(nx):
            for j in range(ny):
                di, dj = move(i)
                if 0 <= i + di < nx and 0 <= j + dj < ny:
                    pairs.append((i * ny + j, (i + di) * ny + j + dj))
        return lax.ppermute(x, axes, pairs)

    x_down = lambda i: (-1, 0)
    x_up = lambda i: (1, 0)
    y_send = lambda i: (0, 1 if i % 2 else -1)
    y_back = lambda i: (0, -1 if i % 2 else 1)

    blocks, couple, inverse, values = face_block[0, 0], coupling[0, 0], interior_inverse[0, 0], face_values[0, 0]
    adj = adjacency[0, 0]
    send = jnp.stack([2 + odd, jnp.int32(0)]).astype(jnp.int32)
    keep = jnp.stack([3 - odd, jnp.int32(1)]).astype(jnp.int32)
    v_send = jnp.where(odd > 0, values[3], values[2])
    v_keep = jnp.stack([jnp.where(odd > 0, values[2], values[3]), values[1]])
    nb = jnp.stack([shift(v_send, y_send), shift(values[0], x_down)])
    (s_send,) = schur_call(send, couple, inverse, blocks)
    s_nb = jnp.stack([shift(s_send[0], y_send), shift(s_send[1], x_down)])
    s_keep, rhs = schur_call(keep, couple, inverse, blocks, values, nb)
    adj_keep = jnp.stack([jnp.where(odd > 0, adj[2], adj[3]), adj[1]])
    x = solve_call(adj_keep, s_keep, s_nb, rhs, v_keep, nb)
    y_ret = shift(x[0], y_back)
    x_ret = shift(x[1], x_up)
    f0 = jnp.where(adj[0] > 0, x_ret, values[0])
    f1 = x[1]
    f2 = jnp.where(odd > 0, x[0], jnp.where(adj[2] > 0, y_ret, values[2]))
    f3 = jnp.where(odd > 0, jnp.where(adj[3] > 0, y_ret, values[3]), x[0])
    averaged = jnp.stack([f0, f1, f2, f3])

    face_count, face_size, rhs_count = averaged.shape
    primal = hi3(primal_basis[0, 0], averaged.reshape(face_count * face_size, rhs_count), TN)
    rows = primal_map[0, 0]
    size = rows.shape[0]
    step_x = ix - rows // (ny * CB)
    step_y = iy - rows // CB % ny
    window = (step_x * 2 + step_y) * CB + rows % CB
    live = jnp.arange(size, dtype=jnp.int32) < primal_count[0, 0]
    hot = ((window[:, None] == jnp.arange(4 * CB, dtype=jnp.int32)[None, :]) & live[:, None]).astype(F32)
    terms = hi3(hot, primal, TN).reshape(4, CB, rhs_count)
    xy_down = lambda i: (-1, -1)
    xy_up = lambda i: (1, 1)
    y_down = lambda i: (0, -1)
    y_up = lambda i: (0, 1)

    def gather_terms(t):
        return t[0] + shift(t[1], y_down) + shift(t[2], x_down) + shift(t[3], xy_down)

    own = gather_terms(terms)
    wide = jnp.concatenate([own, shift(own, y_up), shift(own, x_up), shift(own, xy_up)], axis=0)
    picked = hi3(hot, wide)
    local = hi3(primal_matrix[0, 0], picked)
    product = gather_terms(hi3(hot, local, TN).reshape(4, CB, rhs_count))
    return (averaged[None, None], product)


def solution(mesh):
    in_specs = (
        P("gx", "gy", None, None, None),
        P("gx", "gy", None, None, None),
        P("gx", "gy", None, None),
        P("gx", "gy", None, None, None),
        P("gx", "gy", None),
        P("gx", "gy", None, None),
        P("gx", "gy", None, None),
        P("gx", "gy", None),
        P("gx", "gy"),
    )
    out_specs = (P("gx", "gy", None, None, None), P(("gx", "gy"), None))
    return jax.shard_map(shards, mesh=mesh, in_specs=in_specs, out_specs=out_specs, check_vma=False)
```

```python
import functools

import jax
import jax.numpy as jnp
from jax import lax
from jax.experimental import pallas as pl
from jax.experimental.pallas import tpu as pltpu
from jax.sharding import PartitionSpec as P

CB = 128
TILE = 256
NB = 128
GROUP = 2
F32 = jnp.float32
BF16 = jnp.bfloat16
NN = (((1,), (0,)), ((), ()))
NT = (((1,), (1,)), ((), ()))
MESH = pl.DeviceIdType.MESH
ANY = pl.BlockSpec(memory_space=pl.ANY)
WHOLE = pl.BlockSpec(memory_space=pltpu.VMEM)
SCALARS = pl.BlockSpec(memory_space=pltpu.SMEM)


def halves(x):
    hi = x.astype(BF16)
    lo = (x - hi.astype(F32)).astype(BF16)
    return hi, lo


def mul(a, b, dims=NN):
    return lax.dot_general(a, b, dims, preferred_element_type=F32)


def dot3(a, b, dims=NN):
    ah, al = a if isinstance(a, tuple) else halves(a)
    bh, bl = b if isinstance(b, tuple) else halves(b)
    return mul(ah, bh, dims) + (mul(ah, bl, dims) + mul(al, bh, dims))


def place():
    ix, iy = lax.axis_index("gx"), lax.axis_index("gy")
    nx, ny = lax.axis_size("gx"), lax.axis_size("gy")

    def at(dx, dy):
        return (lax.rem(ix + dx + nx, nx), lax.rem(iy + dy + ny, ny))

    return ix, iy, nx, ny, at


def greet(devices):
    barrier = pltpu.get_barrier_semaphore()
    for device in devices:
        pl.semaphore_signal(barrier, inc=1, device_id=device, device_id_type=MESH)
    pl.semaphore_wait(barrier, len(devices))


def remote(src, dst, send_sem, recv_sem, device):
    return pltpu.make_async_remote_copy(
        src_ref=src, dst_ref=dst, send_sem=send_sem, recv_sem=recv_sem, device_id=device, device_id_type=MESH
    )


def schur_into(out_ref, a_ref, c_hi, c_lo, t_hi, t_lo, acc):
    width = c_hi.shape[1]
    for j in range(width // TILE):
        cols = slice(j * TILE, (j + 1) * TILE)
        rest = slice(j * TILE, width)
        w = dot3((c_hi[:, rest], c_lo[:, rest]), (t_hi[rest, cols], t_lo[rest, cols]))
        part = dot3(w, (c_hi[:, cols], c_lo[:, cols]), NT)
        if j == 0:
            acc[...] = part
        else:
            acc[...] += part
    x = acc[...]
    out_ref[...] = a_ref[...] - (x + x.T)


def schur_kernel(
    c_any, k_any, a_any, v_ref,
    m_ref, rhs_ref, nb_ref,
    k_ref, c_ref, a_ref, t_hi, t_lo, c_hi, c_lo, acc, s_ref, r_ref,
    k_sem, c_sem, a_sem, vs_sem, vr_sem, ss_sem, sr_sem,
):
    ix, iy, nx, ny, at = place()
    odd = lax.rem(ix, 2)
    step = 2 * odd - 1
    to = (at(0, step), at(-1, 0))
    size, width = c_hi.shape
    tiles = width // TILE
    half = size // 2
    faces = (2 + odd, 0, 3 - odd, 1)

    def k_copy(i):
        rows, cols = pl.ds(i * TILE, TILE), pl.ds(0, (i + 1) * TILE)
        return pltpu.make_async_copy(k_any.at[0, 0, rows, cols], k_ref.at[rows, cols], k_sem.at[i])

    def c_copy(s):
        return pltpu.make_async_copy(c_any.at[0, 0, faces[s]], c_ref.at[s % 2], c_sem.at[s % 2])

    def a_copy(s):
        return pltpu.make_async_copy(a_any.at[0, 0, faces[s]], a_ref.at[s % 2], a_sem.at[s % 2])

    c_copy(0).start()
    for i in reversed(range(tiles)):
        k_copy(i).start()
    a_copy(0).start()
    c_copy(1).start()
    a_copy(1).start()
    greet((at(0, 1), at(0, -1), at(1, 0), at(-1, 0)))
    v_copies = [remote(v_ref.at[0, 0, faces[s]], nb_ref.at[s], vs_sem.at[s], vr_sem.at[s], to[s]) for s in range(2)]
    for copy in v_copies:
        copy.start()

    parts = ((pl.ds(half, half), pl.ds(0, size)), (pl.ds(0, half), pl.ds(0, half)))
    s_copies = [
        [remote(s_ref.at[(s, *part)], r_ref.at[(s, *part)], ss_sem.at[s, n], sr_sem.at[s, n], to[s]) for n, part in enumerate(parts)]
        for s in range(2)
    ]
    c_copy(0).wait()
    c_hi[...], c_lo[...] = halves(c_ref[0])
    for i in reversed(range(tiles)):
        k_copy(i).wait()
        for j in range(i + 1):
            rows, cols = slice(i * TILE, (i + 1) * TILE), slice(j * TILE, (j + 1) * TILE)
            t = k_ref[rows, cols]
            t_hi[rows, cols], t_lo[rows, cols] = halves(0.5 * t if i == j else t)
    for s in range(4):
        if s > 0:
            c_copy(s).wait()
            c_hi[...], c_lo[...] = halves(c_ref[s % 2])
        a_copy(s).wait()
        out = s_ref.at[s] if s < 2 else m_ref.at[s - 2]
        schur_into(out, a_ref.at[s % 2], c_hi, c_lo, t_hi, t_lo, acc)
        if s < 2:
            c_copy(s + 2).start()
            a_copy(s + 2).start()
            for copy in s_copies[s]:
                copy.start()
        else:
            f = s - 2
            v_copies[f].wait()
            rhs_ref[f] = dot3(m_ref[f], v_ref[0, 0, faces[s]] - nb_ref[f])
    for f in range(2):
        for copy in s_copies[f]:
            copy.wait()
        m_ref[f, :half, :half] += r_ref[f, :half, :half]
        low = r_ref[f, half:, :]
        m_ref[f, half:, :] += low
        m_ref[f, :half, half:] += low[:, :half].T


def schur_call(couple, inverse, blocks, values):
    size, width = couple.shape[3:]
    rhs = values.shape[4]
    dma = pltpu.SemaphoreType.DMA
    return pl.pallas_call(
        schur_kernel,
        in_specs=[ANY, ANY, ANY, WHOLE],
        out_specs=[WHOLE] * 3,
        out_shape=[
            jax.ShapeDtypeStruct((2, size, size), F32),
            jax.ShapeDtypeStruct((2, size, rhs), F32),
            jax.ShapeDtypeStruct((2, size, rhs), F32),
        ],
        scratch_shapes=[
            pltpu.VMEM((width, width), F32),
            pltpu.VMEM((2, size, width), F32),
            pltpu.VMEM((2, size, size), F32),
            pltpu.VMEM((width, width), BF16),
            pltpu.VMEM((width, width), BF16),
            pltpu.VMEM((size, width), BF16),
            pltpu.VMEM((size, width), BF16),
            pltpu.VMEM((size, size), F32),
            pltpu.VMEM((2, size, size), F32),
            pltpu.VMEM((2, size, size), F32),
            dma((width // TILE,)), dma((2,)), dma((2,)), dma((2,)), dma((2,)), dma((2, 2)), dma((2, 2)),
        ],
        compiler_params=pltpu.CompilerParams(collective_id=1, has_side_effects=True),
        name="schur",
    )(couple, inverse, blocks, values)


def lane(x, k):
    return jnp.broadcast_to(x[:, :, k : k + 1], x.shape)


def sub(x, k):
    return jnp.broadcast_to(x[:, k : k + 1, :], x.shape)


def stacked(left):
    return jnp.concatenate(halves(left), axis=1)


def doubled(hi, lo):
    return jnp.concatenate(
        [jnp.concatenate([hi, lo], axis=1), jnp.concatenate([hi, jnp.zeros_like(lo)], axis=1)], axis=0
    )


def prod3(left, right):
    out = mul(stacked(left), doubled(*halves(right)), NN)
    n = right.shape[1]
    return out[:, :n] + out[:, n:]


def eliminate_panel(tiles, p, base, rows, cols):
    start = 8 * (base + p)
    span = (cols >= start) & (cols < start + 8)
    others = [q for q in range(p + 1, len(tiles))] + [q for q in range(p)]
    c = [lane(tiles[p], start + j) for j in range(8)]
    g = {q: [lane(tiles[q], start + j) for j in range(8)] for q in others}
    u = jnp.where(span, jnp.where(cols - start == rows, 1.0, 0.0), tiles[p])
    for j in range(8):
        r = sub(1.0 / c[j], j)
        f = jnp.where(rows == j, 1.0 - r, c[j] * r)
        for m in range(j + 1, 8):
            c[m] = c[m] - f * sub(c[m], j)
        u = u - f * sub(u, j)
    u_rows = [sub(u, j) for j in range(8)]
    for q in others:
        terms = [g[q][j] * u_rows[j] for j in range(8)]
        while len(terms) > 1:
            terms = [terms[i] + terms[i + 1] for i in range(0, len(terms), 2)]
        tiles[q] = jnp.where(span, 0.0, tiles[q]) - terms[0]
    tiles[p] = u


def invert(tiles, side_work):
    faces, _, n = tiles[0].shape
    shape = tiles[0].shape
    rows = lax.broadcasted_iota(jnp.int32, shape, 1)
    cols = lax.broadcasted_iota(jnp.int32, shape, 2)
    count = len(tiles)
    for base in range(0, count, GROUP):
        mine = tiles[base : base + GROUP]
        rest = [q for q in range(count) if not base <= q < base + GROUP]
        left = [stacked(jnp.concatenate([tiles[q][f] for q in rest], axis=0)) for f in range(faces)]
        for p in range(GROUP):
            eliminate_panel(mine, p, base, rows, cols)
            if side_work:
                side_work.pop(0)()
        span = (cols >= 8 * base) & (cols < 8 * (base + GROUP))
        out = []
        for f in range(faces):
            v = jnp.concatenate([m[f] for m in mine], axis=0)
            hi, lo = halves(v)
            wide = jnp.concatenate([jnp.concatenate([hi, lo], axis=1), jnp.concatenate([hi, jnp.zeros_like(lo)], axis=1)], axis=0)
            zero = lambda m: jnp.zeros((m, 2 * n), BF16)
            top, low = 8 * base, n - 8 * (base + GROUP)
            one = lambda part: [zero(top)] * (top > 0) + [part] + [zero(low)] * (low > 0)
            half = 8 * GROUP
            right = jnp.concatenate(one(wide[:half]) + one(wide[half:]), axis=0)
            o = mul(left[f], right, NN)
            out.append(o[:, :n] + o[:, n:])
        for i, q in enumerate(rest):
            upd = jnp.stack([out[f][8 * i : 8 * i + 8] for f in range(faces)])
            tiles[q] = jnp.where(span, 0.0, tiles[q]) - upd
        tiles[base : base + GROUP] = mine
    while side_work:
        side_work.pop(0)()


def solve_kernel(s_ref, rhs_ref, nb_ref, x_ref, m_ref, hi_ref, lo_ref):
    faces, size, width = rhs_ref.shape
    count = size // NB
    total = size + width
    m_ref[:, :, :size] = s_ref[...]
    m_ref[:, :, size:] = rhs_ref[...]
    side_work = []
    for k in range(count):
        rk = slice(k * NB, (k + 1) * NB)
        tiles = [m_ref[:, k * NB + 8 * q : k * NB + 8 * q + 8, rk] for q in range(NB // 8)]
        invert(tiles, side_work)
        inv = [stacked(jnp.concatenate([t[f] for t in tiles], axis=0)) for f in range(faces)]

        def scale(f, cols, inv=inv, rk=rk):
            hi, lo = halves(m_ref[f, rk, cols])
            out = mul(inv[f], jnp.concatenate([hi, hi], axis=0), NN) + mul(inv[f][:, :NB], lo, NN)
            m_ref[f, rk, cols] = out
            hi_ref[f, :, cols], lo_ref[f, :, cols] = halves(out)

        def update(f, i, cols, rk=rk):
            ri = slice(i * NB, (i + 1) * NB)
            left = stacked(m_ref[f, ri, rk])
            hi = hi_ref[f, :, cols]
            m_ref[f, ri, cols] -= mul(left, jnp.concatenate([hi, hi], axis=0), NN) + mul(
                left[:, :NB], lo_ref[f, :, cols], NN
            )

        if k < count - 1:
            near = slice((k + 1) * NB, (k + 2) * NB)
            far = slice((k + 2) * NB, total)
            for f in range(faces):
                scale(f, near)
            for f in range(faces):
                update(f, k + 1, near)
            side_work += [functools.partial(scale, f, far) for f in range(faces)]
            side_work += [functools.partial(update, f, k + 1, far) for f in range(faces)]
            for i in range(count):
                if i not in (k, k + 1):
                    side_work += [functools.partial(update, f, i, slice((k + 1) * NB, total)) for f in range(faces)]
        else:
            for f in range(faces):
                scale(f, slice(size, total))
                for i in range(count - 1):
                    update(f, i, slice(size, total))
    for f in range(faces):
        x_ref[f] = nb_ref[f] + m_ref[f, :, size:]


def solve_call(m, rhs, nb):
    _, size, width = rhs.shape
    return pl.pallas_call(
        solve_kernel,
        in_specs=[WHOLE] * 3,
        out_specs=WHOLE,
        out_shape=jax.ShapeDtypeStruct((2, size, width), F32),
        scratch_shapes=[
            pltpu.VMEM((2, size, size + width), F32),
            pltpu.VMEM((2, NB, size + width), BF16),
            pltpu.VMEM((2, NB, size + width), BF16),
        ],
        name="solve",
    )(m, rhs, nb)


def coarse_kernel(
    count_ref, adj_ref, map_ref, x_ref, v_ref, basis_any, matrix_any,
    avg_any, out_ref,
    avg, basis, matrix, ret, outgoing, incoming,
    b_sem, m_sem, o_sem, rs_sem, rr_sem, s_sem, r_sem,
):
    ix, iy, nx, ny, at = place()
    odd = lax.rem(ix, 2)
    step = 2 * odd - 1
    size, rhs = x_ref.shape[1:]
    primal = matrix.shape[0]
    b_copy = pltpu.make_async_copy(basis_any.at[0, 0], basis, b_sem)
    m_copy = pltpu.make_async_copy(matrix_any.at[0, 0], matrix, m_sem)
    b_copy.start()
    m_copy.start()
    down = (at(0, -1), at(-1, 0), at(-1, -1))
    up = (at(0, 1), at(1, 0), at(1, 1))
    greet(down + up)
    back = (at(0, -step), at(1, 0))
    returns = [remote(x_ref.at[f], ret.at[f], rs_sem.at[f], rr_sem.at[f], back[f]) for f in range(2)]
    for copy in returns:
        copy.start()

    own, other = 3 - odd, 2 + odd

    def out_copy(face, n):
        return pltpu.make_async_copy(avg.at[face], avg_any.at[0, 0, face], o_sem.at[n])

    def glued(f, face, new):
        avg[face] = jnp.where(adj_ref[0, 0, face] > 0, new, v_ref[0, 0, face])
        out_copy(face, f).start()

    glued(0, own, x_ref[0])
    glued(1, 1, x_ref[1])
    rows = map_ref[0]
    window = ((ix - (rows >> 11)) * 2 + iy - ((rows >> 7) & 15)) * CB + (rows & 127)
    live = lax.broadcasted_iota(jnp.int32, rows.shape, 1) < count_ref[0, 0]
    window = jnp.where(live, window, -1)
    spots = lax.broadcasted_iota(jnp.int32, (4 * CB, primal), 0)
    hot = jnp.where(spots == window, 1.0, 0.0).astype(BF16)
    b_copy.wait()

    def part(face):
        start = face * size
        if not isinstance(face, int):
            start = pl.multiple_of(start, size)
        return dot3(avg[face].T, basis[pl.ds(start, size), :])

    total = part(own) + part(1)
    m_copy.wait()
    mh, ml = halves(matrix[...])
    for copy in returns:
        copy.wait()
    glued(2, other, ret[0])
    glued(3, 0, ret[1])
    total += part(other) + part(0)

    def spread(x):
        hi, lo = halves(x)
        return mul(hi, hot, NT) + mul(lo, hot, NT)

    def blocks(n, devices, arrays):
        copies = []
        for b in range(3):
            outgoing[n, b] = arrays[b]
            copies.append(remote(outgoing.at[n, b], incoming.at[n, b], s_sem.at[n, b], r_sem.at[n, b], devices[b]))
            copies[b].start()
        return copies

    inside_x, inside_y = ix < nx - 1, iy < ny - 1

    def assemble(n, terms):
        copies = blocks(n, down, [terms[:, b * CB : (b + 1) * CB] for b in range(1, 4)])
        for copy in copies:
            copy.wait()
        return (
            terms[:, :CB]
            + jnp.where(inside_y, incoming[n, 0], 0.0)
            + jnp.where(inside_x, incoming[n, 1], 0.0)
            + jnp.where(jnp.logical_and(inside_x, inside_y), incoming[n, 2], 0.0)
        )

    residual = assemble(0, spread(total))
    copies = blocks(1, up, [residual] * 3)
    for copy in copies:
        copy.wait()
    wide = jnp.concatenate([residual, incoming[1, 0], incoming[1, 1], incoming[1, 2]], axis=1)
    hi, lo = halves(wide)
    picked = mul(hi, hot) + mul(lo, hot)
    local = dot3(picked, (mh, ml), NT)
    out_ref[...] = assemble(2, spread(local)).T
    for n, face in enumerate((own, 1, other, 0)):
        out_copy(face, n).wait()


def coarse_call(count, adjacency, rows, x, values, basis, matrix):
    size, rhs = x.shape[1:]
    primal = matrix.shape[2]
    dma = pltpu.SemaphoreType.DMA
    return pl.pallas_call(
        coarse_kernel,
        in_specs=[SCALARS, SCALARS, WHOLE, WHOLE, WHOLE, ANY, ANY],
        out_specs=[ANY, WHOLE],
        out_shape=[jax.ShapeDtypeStruct(values.shape, F32), jax.ShapeDtypeStruct((CB, rhs), F32)],
        scratch_shapes=[
            pltpu.VMEM(values.shape[2:], F32),
            pltpu.VMEM(basis.shape[2:], F32),
            pltpu.VMEM((primal, primal), F32),
            pltpu.VMEM((2, size, rhs), F32),
            pltpu.VMEM((3, 3, rhs, CB), F32),
            pltpu.VMEM((3, 3, rhs, CB), F32),
            dma, dma, dma((4,)), dma((2,)), dma((2,)), dma((3, 3)), dma((3, 3)),
        ],
        compiler_params=pltpu.CompilerParams(collective_id=2, has_side_effects=True),
        name="coarse",
    )(count, adjacency, rows, x, values, basis, matrix)


def shards(
    face_block,
    coupling,
    interior_inverse,
    face_values,
    adjacency,
    primal_basis,
    primal_matrix,
    primal_map,
    primal_count,
):
    m, rhs, nb = schur_call(coupling, interior_inverse, face_block, face_values)
    x = solve_call(m, rhs, nb)
    return coarse_call(primal_count, adjacency, primal_map, x, face_values, primal_basis, primal_matrix)


def solution(mesh):
    in_specs = (
        P("gx", "gy", None, None, None),
        P("gx", "gy", None, None, None),
        P("gx", "gy", None, None),
        P("gx", "gy", None, None, None),
        P("gx", "gy", None),
        P("gx", "gy", None, None),
        P("gx", "gy", None, None),
        P("gx", "gy", None),
        P("gx", "gy"),
    )
    out_specs = (P("gx", "gy", None, None, None), P(("gx", "gy"), None))
    return jax.shard_map(shards, mesh=mesh, in_specs=in_specs, out_specs=out_specs, check_vma=False)
```
